32 devices in a mesh: groups: 2 (over y), seq: 8 (over z, x), head: 2 (over core).
Axes of the slice: x: 2, y: 2, z: 4, core: 2. Of those that a mesh axis runs over, the one named last changes fastest.
Arguments:
- queries: bfloat16 [256, 3072], P(('groups', 'seq'), 'head'), parts along dimension 0, may hold values from -300 to 300, as said below
- latent: bfloat16 [512, 256], P(None, ('groups', 'seq')), parts along dimension 1, may hold values from -6 to 6
- key_basis: bfloat16 [512, 3072], P(None, 'head'), may hold values from -0.25 to 0.25
- value_basis: bfloat16 [512, 3072], P(None, 'head'), may hold values from -0.25 to 0.25
- out_weight: bfloat16 [3072, 3072], P('seq', 'head'), may hold values from -0.625 to 0.625
Outputs:
- attended: bfloat16 [256, 3072], P(('groups', 'seq'), 'head'), parts along dimension 0
The draws below stay inside these ranges and needn't reach their ends.
There are 2 independent parts, one for each index of `groups`. The reference program is written for one: setup_inputs(seed, part) draws one part's arguments, and reference() takes and returns one part's arrays. A program takes and returns all parts, laid end to end along the dimension named above; an argument that names none is the same for every part. Nothing has to cross between parts.
Inputs may be any that keep to these rules, and one draw needn't show every extreme that they name: `queries`: real-valued entries.
All inputs are finite; a program needn't handle non-finite values.
Results may differ from the reference program's by a relative error of at most 0.0099.
Values may be sent and summed in bfloat16 or wider, within the bound.
A program may use at most 64 MiB of HBM per device.

```python
import math
import jax
import jax.numpy as jnp
from jax import lax

D = 3072
HEADS = 24
HEAD_DIM = 128
RANK = 512
TOKENS = 128


def draw_queries(key, part):
    first = jax.random.fold_in(jax.random.fold_in(key, 11), 0)
    values = jax.random.normal(first, (TOKENS, HEADS * HEAD_DIM), jnp.float32) * 1.4
    return jnp.clip(values, -300.0, 300.0).astype(jnp.bfloat16)


def levels(stream_key, extent, shards, least, top_value):
    def one(position, parts):
        draws = jax.random.uniform(jax.random.fold_in(jax.random.fold_in(stream_key, 6), position), (parts,), jnp.float32, least / len(shards), top_value / len(shards))
        return jnp.repeat(jnp.exp(draws), extent[position] // parts).reshape((-1,) + (1,) * (len(extent) - position - 1))

    loudness = one(*shards[0])
    for cut in shards[1:]:
        loudness = loudness * one(*cut)
    return loudness


def gaussian(rng, extent, scale, reach, cuts=(), kind=jnp.bfloat16):
    level = levels(rng, extent, cuts, -0.22, 0.18) if cuts else 1.0
    drawn = jax.random.normal(rng, extent, jnp.float32) * scale * level
    return jnp.minimum(jnp.maximum(drawn, -reach), reach).astype(kind)


def setup_inputs(seed: int = 0, part: int = 0) -> dict:
    splits = jax.random.split(jax.random.key(seed), 6)
    part_splits = jax.random.split(jax.random.fold_in(splits[5], part), 6)
    queries = draw_queries(jax.random.fold_in(jax.random.fold_in(splits[5], part), 71), part)
    latent = gaussian(part_splits[1], (RANK, TOKENS), 1.0, 6.0, ((1, 8),))
    key_basis = gaussian(splits[2], (RANK, HEADS * HEAD_DIM), RANK ** -0.5, 0.25, ((1, 2),))
    value_basis = gaussian(splits[3], (RANK, HEADS * HEAD_DIM), RANK ** -0.5, 0.25, ((1, 2),))
    out_weight = gaussian(splits[4], (D, HEADS * HEAD_DIM), (HEADS * HEAD_DIM // 32) ** -0.5, 0.625, ((0, 8), (1, 2)))
    return {"queries": queries, "latent": latent, "key_basis": key_basis, "value_basis": value_basis, "out_weight": out_weight}


def attend(queries, latent, key_basis, value_basis):
    tok_rows = queries.shape[0]
    head_count = key_basis.shape[1] // HEAD_DIM
    rank_count = key_basis.shape[0]
    score_scale = 1.0 / math.sqrt(HEAD_DIM)
    query_heads = queries.reshape(tok_rows, head_count, HEAD_DIM).transpose(1, 0, 2)
    key_maps = key_basis.reshape(rank_count, head_count, HEAD_DIM).transpose(1, 0, 2)
    value_maps = value_basis.reshape(rank_count, head_count, HEAD_DIM).transpose(1, 0, 2)

    def one_head(operands):
        query_one, key_map, value_map = operands
        key_rows = lax.dot_general(latent, key_map, (((0,), (0,)), ((), ())), preferred_element_type=jnp.float32).astype(jnp.bfloat16)
        value_rows = lax.dot_general(latent, value_map, (((0,), (0,)), ((), ())), preferred_element_type=jnp.float32).astype(jnp.bfloat16)
        scores = lax.dot_general(query_one, key_rows, (((1,), (1,)), ((), ())), preferred_element_type=jnp.float32) * score_scale
        row_max = lax.optimization_barrier(jnp.max(scores, axis=1, keepdims=True))
        weights = jnp.exp(scores - row_max)
        row_total = lax.optimization_barrier(jnp.sum(weights, axis=1, keepdims=True))
        head_mixed = jnp.dot(weights.astype(jnp.bfloat16), value_rows, preferred_element_type=jnp.float32) / row_total
        return head_mixed.astype(jnp.bfloat16)
    mixed = lax.map(one_head, (query_heads, key_maps, value_maps))
    return mixed.transpose(1, 0, 2).reshape(tok_rows, head_count * HEAD_DIM)

def reference(queries, latent, key_basis, value_basis, out_weight):
    mixed = attend(queries, latent, key_basis, value_basis)
    attended = lax.dot_general(mixed, out_weight, (((1,), (1,)), ((), ())), preferred_element_type=jnp.float32)
    return attended.astype(jnp.bfloat16)
```

```python
import functools
import math

import jax
import jax.numpy as jnp
from jax import lax
from jax.experimental import pallas as pl
from jax.experimental.pallas import tpu as pltpu
from jax.sharding import PartitionSpec as P

HEAD_DIM = 128
MESH = pl.DeviceIdType.MESH
VMEM_BUDGET = 40 * 2**20


def attend(queries, latent, key_basis, value_basis):
    tok_rows = queries.shape[0]
    head_count = key_basis.shape[1] // HEAD_DIM
    rank_count = key_basis.shape[0]
    score_scale = 1.0 / math.sqrt(HEAD_DIM)
    query_heads = queries.reshape(tok_rows, head_count, HEAD_DIM).transpose(1, 0, 2)
    key_maps = key_basis.reshape(rank_count, head_count, HEAD_DIM).transpose(1, 0, 2)
    value_maps = value_basis.reshape(rank_count, head_count, HEAD_DIM).transpose(1, 0, 2)

    def one_head(operands):
        query_one, key_map, value_map = operands
        key_rows = lax.dot_general(
            latent, key_map, (((0,), (0,)), ((), ())), preferred_element_type=jnp.float32
        ).astype(jnp.bfloat16)
        value_rows = lax.dot_general(
            latent, value_map, (((0,), (0,)), ((), ())), preferred_element_type=jnp.float32
        ).astype(jnp.bfloat16)
        scores = (
            lax.dot_general(
                query_one, key_rows, (((1,), (1,)), ((), ())), preferred_element_type=jnp.float32
            )
            * score_scale
        )
        row_max = jnp.max(scores, axis=1, keepdims=True)
        weights = jnp.exp(scores - row_max)
        row_total = jnp.sum(weights, axis=1, keepdims=True)
        head_mixed = (
            jnp.dot(weights.astype(jnp.bfloat16), value_rows, preferred_element_type=jnp.float32)
            / row_total
        )
        return head_mixed.astype(jnp.bfloat16)

    mixed = lax.map(one_head, (query_heads, key_maps, value_maps))
    return mixed.transpose(1, 0, 2).reshape(tok_rows, head_count * HEAD_DIM)


def collective_shards(queries, latent, key_basis, value_basis, out_weight):
    gathered = lax.all_gather(latent, "seq", axis=1, tiled=True)
    attended_heads = attend(queries, gathered, key_basis, value_basis)
    partial_value = lax.dot_general(
        attended_heads,
        lax.all_gather(out_weight, "seq", axis=0, tiled=True),
        (((1,), (1,)), ((), ())),
        preferred_element_type=jnp.float32,
    )
    return lax.psum_scatter(partial_value, "head", scatter_dimension=1, tiled=True).astype(
        jnp.bfloat16
    )


def chunk_count(heads):
    return next(c for c in (4, 3, 2, 1) if heads % c == 0)


def kernel(
    n,
    q_hbm, lat_hbm, kb_hbm, vb_hbm, ow_hbm,
    out_ref,
    q_all, lat_all, kb, vb, ow, keys, values, part, swap, fin, landed,
    local_sem, send_sem, recv_sem, swap_sem, fin_send, fin_recv,
):
    chunks, _, tok, width = q_all.shape
    tokens = n * tok
    rows = n // 2
    heads = width // HEAD_DIM
    score_scale = 1.0 / math.sqrt(HEAD_DIM)
    me, core = lax.axis_index("seq"), lax.axis_index("head")
    row, side = me // 2, me % 2
    partner = row * 2 + (1 - side)

    def column(j, which=side):
        return ((row + j) % rows) * 2 + which

    def to(seq, head=core):
        return {"seq": seq, "head": head}

    locals_ = [
        pltpu.make_async_copy(lat_hbm, lat_all.at[me], local_sem.at[0]),
        pltpu.make_async_copy(kb_hbm, kb, local_sem.at[1]),
        pltpu.make_async_copy(vb_hbm, vb, local_sem.at[2]),
        pltpu.make_async_copy(ow_hbm, ow, local_sem.at[3]),
    ] + [
        pltpu.make_async_copy(
            q_hbm.at[:, pl.ds(c * width, width)], q_all.at[c, me], local_sem.at[4 + c]
        )
        for c in range(chunks)
    ]
    for copy in locals_:
        copy.start()

    barrier = pltpu.get_barrier_semaphore()
    greet = [to(column(j)) for j in range(1, rows)] + [to(partner), to(me, 1 - core)]
    for peer in greet:
        pl.semaphore_signal(barrier, inc=1, device_id=peer, device_id_type=MESH)
    pl.semaphore_wait(barrier, len(greet))

    started = []

    def piece(c, seq):
        return lat_all.at[seq] if c == chunks else q_all.at[c, seq]

    def send(c, src, seq, target, slot):
        copy = pltpu.make_async_remote_copy(
            src_ref=src,
            dst_ref=piece(c, seq),
            send_sem=send_sem.at[c, slot],
            recv_sem=recv_sem.at[c, seq],
            device_id=target,
            device_id_type=MESH,
        )
        copy.start()
        started.append(copy)

    def arrived(c, seq):
        pltpu.make_async_remote_copy(
            src_ref=piece(c, seq),
            dst_ref=piece(c, seq),
            send_sem=send_sem.at[c, 0],
            recv_sem=recv_sem.at[c, seq],
            device_id=to(partner),
            device_id_type=MESH,
        ).wait_recv()

    def spread(c, src):
        for j in range(1, rows):
            send(c, src, me, to(column(j)), j)
        send(c, src, me, to(partner), 0)

    def relay(c):
        for j in range(1, rows):
            arrived(c, column(j))
            send(c, piece(c, column(j)), column(j), to(partner), rows - 1 + j)

    spread(chunks, lat_hbm)
    for c in range(chunks):
        spread(c, q_hbm.at[:, pl.ds(c * width, width)])

    relay(chunks)
    for j in range(rows):
        arrived(chunks, column(j, 1 - side))
    locals_[0].wait()
    latent = lat_all[...].reshape(tokens, lat_all.shape[2])
    locals_[1].wait()
    locals_[2].wait()
    for c in range(chunks):
        cols = pl.ds(c * width, width)
        keys[c] = jnp.dot(latent, kb[:, cols], preferred_element_type=jnp.float32).astype(
            jnp.bfloat16
        )
        values[c] = jnp.dot(latent, vb[:, cols], preferred_element_type=jnp.float32).astype(
            jnp.bfloat16
        )
        relay(c)

    locals_[3].wait()
    total = None
    for c in range(chunks):
        for j in range(rows):
            arrived(c, column(j, 1 - side))
        locals_[4 + c].wait()
        mixed = []
        for h in range(heads):
            cols = pl.ds(h * HEAD_DIM, HEAD_DIM)
            query = q_all[c, :, :, cols].reshape(tokens, HEAD_DIM)
            scores = (
                lax.dot_general(
                    query,
                    keys[c, :, cols],
                    (((1,), (1,)), ((), ())),
                    preferred_element_type=jnp.float32,
                )
                * score_scale
            )
            weights = jnp.exp(scores - jnp.max(scores, axis=1, keepdims=True))
            totals = jnp.sum(weights, axis=1, keepdims=True)
            mixed.append(
                (
                    jnp.dot(
                        weights.astype(jnp.bfloat16),
                        values[c, :, cols],
                        preferred_element_type=jnp.float32,
                    )
                    / totals
                ).astype(jnp.bfloat16)
            )
        term = lax.dot_general(
            jnp.concatenate(mixed, axis=1) if heads > 1 else mixed[0],
            ow[:, pl.ds(c * width, width)],
            (((1,), (1,)), ((), ())),
            preferred_element_type=jnp.float32,
        )
        total = term if total is None else total + term

    part[...] = total.reshape(part.shape)
    exchange = pltpu.make_async_remote_copy(
        src_ref=part.at[1 - core],
        dst_ref=swap,
        send_sem=swap_sem.at[0],
        recv_sem=swap_sem.at[1],
        device_id=to(me, 1 - core),
        device_id_type=MESH,
    )
    exchange.start()
    exchange.wait_recv()
    fin[...] = (part[core] + swap[...]).astype(jnp.bfloat16).reshape(fin.shape)

    slot, keeper = me % rows, me // rows
    for j in range(rows):
        owner = core * rows + j
        here = jnp.logical_and(owner == me, keeper == core)
        copy = pltpu.make_async_remote_copy(
            src_ref=fin.at[j],
            dst_ref=landed.at[slot],
            send_sem=fin_send.at[j],
            recv_sem=fin_recv.at[slot],
            device_id=to(owner, keeper),
            device_id_type=MESH,
        )

        @pl.when(jnp.logical_not(here))
        def _():
            copy.start()

        @pl.when(here)
        def _():
            landed[slot] = fin[j]

    own_here = me // rows == core
    feats = landed.shape[2]
    for i in range(rows):
        @pl.when(jnp.logical_not(jnp.logical_and(own_here, i == slot)))
        def _():
            pltpu.make_async_remote_copy(
                src_ref=landed.at[i],
                dst_ref=landed.at[i],
                send_sem=fin_send.at[0],
                recv_sem=fin_recv.at[i],
                device_id=to(partner),
                device_id_type=MESH,
            ).wait_recv()

        out_ref[:, i * feats : (i + 1) * feats] = landed[i]

    for copy in started:
        copy.wait_send()
    exchange.wait_send()
    for j in range(rows):
        owner = core * rows + j

        @pl.when(jnp.logical_not(jnp.logical_and(owner == me, keeper == core)))
        def _():
            pltpu.make_async_remote_copy(
                src_ref=fin.at[j],
                dst_ref=landed.at[slot],
                send_sem=fin_send.at[j],
                recv_sem=fin_recv.at[slot],
                device_id=to(owner, keeper),
                device_id_type=MESH,
            ).wait_send()


def fused_shards(n, queries, latent, key_basis, value_basis, out_weight):
    tok, local = queries.shape
    rank = latent.shape[0]
    feats = out_weight.shape[0]
    chunks = chunk_count(local // HEAD_DIM)
    width = local // chunks
    rows = n // 2
    tokens = n * tok
    bf16, f32 = jnp.bfloat16, jnp.float32
    hbm = pl.BlockSpec(memory_space=pl.ANY)
    return pl.pallas_call(
        functools.partial(kernel, n),
        out_shape=jax.ShapeDtypeStruct((tok, rows * feats), bf16),
        in_specs=[hbm] * 5,
        out_specs=pl.BlockSpec(memory_space=pltpu.VMEM),
        scratch_shapes=[
            pltpu.VMEM((chunks, n, tok, width), bf16),
            pltpu.VMEM((n, tok, rank), bf16),
            pltpu.VMEM((rank, local), bf16),
            pltpu.VMEM((rank, local), bf16),
            pltpu.VMEM((feats, local), bf16),
            pltpu.VMEM((chunks, tokens, width), bf16),
            pltpu.VMEM((chunks, tokens, width), bf16),
            pltpu.VMEM((2, tokens // 2, feats), f32),
            pltpu.VMEM((tokens // 2, feats), f32),
            pltpu.VMEM((rows, tok, feats), bf16),
            pltpu.VMEM((rows, tok, feats), bf16),
            pltpu.SemaphoreType.DMA((4 + chunks,)),
            pltpu.SemaphoreType.DMA((chunks + 1, n)),
            pltpu.SemaphoreType.DMA((chunks + 1, n)),
            pltpu.SemaphoreType.DMA((2,)),
            pltpu.SemaphoreType.DMA((rows,)),
            pltpu.SemaphoreType.DMA((rows,)),
        ],
        compiler_params=pltpu.CompilerParams(collective_id=0, has_side_effects=True),
        name="fused_attention",
    )(queries, latent.T, key_basis, value_basis, out_weight)


def shards(n, cores, queries, latent, key_basis, value_basis, out_weight):
    tok, local = queries.shape
    rank = latent.shape[0]
    feats = out_weight.shape[0]
    tokens = n * tok
    held = 2 * (3 * tokens * local + tokens * rank + 2 * rank * local + feats * local)
    held += 4 * (3 * tokens * feats + 3 * tokens * tokens)
    if (
        cores == 2
        and n % 2 == 0
        and tok % 16 == 0
        and feats % 128 == 0
        and rank % 128 == 0
        and held <= VMEM_BUDGET
    ):
        return fused_shards(n, queries, latent, key_basis, value_basis, out_weight)
    return collective_shards(queries, latent, key_basis, value_basis, out_weight)


def solution(mesh):
    placed = (
        P(("groups", "seq"), "head"),
        P(None, ("groups", "seq")),
        P(None, "head"),
        P(None, "head"),
        P("seq", "head"),
    )
    return jax.shard_map(
        functools.partial(shards, mesh.shape["seq"], mesh.shape["head"]),
        mesh=mesh,
        in_specs=placed,
        out_specs=P(("groups", "seq"), "head"),
        check_vma=False,
    )
```

```python
import functools
import math

import jax
import jax.numpy as jnp
from jax import lax
from jax.experimental import pallas as pl
from jax.experimental.pallas import tpu as pltpu
from jax.sharding import PartitionSpec as P

HEAD_DIM = 128
MESH = pl.DeviceIdType.MESH
VMEM_BUDGET = 40 * 2**20
DIRECT = 0


def attend(queries, latent, key_basis, value_basis):
    tok_rows = queries.shape[0]
    head_count = key_basis.shape[1] // HEAD_DIM
    rank_count = key_basis.shape[0]
    score_scale = 1.0 / math.sqrt(HEAD_DIM)
    query_heads = queries.reshape(tok_rows, head_count, HEAD_DIM).transpose(1, 0, 2)
    key_maps = key_basis.reshape(rank_count, head_count, HEAD_DIM).transpose(1, 0, 2)
    value_maps = value_basis.reshape(rank_count, head_count, HEAD_DIM).transpose(1, 0, 2)

    def one_head(operands):
        query_one, key_map, value_map = operands
        key_rows = lax.dot_general(
            latent, key_map, (((0,), (0,)), ((), ())), preferred_element_type=jnp.float32
        ).astype(jnp.bfloat16)
        value_rows = lax.dot_general(
            latent, value_map, (((0,), (0,)), ((), ())), preferred_element_type=jnp.float32
        ).astype(jnp.bfloat16)
        scores = (
            lax.dot_general(
                query_one, key_rows, (((1,), (1,)), ((), ())), preferred_element_type=jnp.float32
            )
            * score_scale
        )
        row_max = jnp.max(scores, axis=1, keepdims=True)
        weights = jnp.exp(scores - row_max)
        row_total = jnp.sum(weights, axis=1, keepdims=True)
        head_mixed = (
            jnp.dot(weights.astype(jnp.bfloat16), value_rows, preferred_element_type=jnp.float32)
            / row_total
        )
        return head_mixed.astype(jnp.bfloat16)

    mixed = lax.map(one_head, (query_heads, key_maps, value_maps))
    return mixed.transpose(1, 0, 2).reshape(tok_rows, head_count * HEAD_DIM)


def collective_shards(queries, latent, key_basis, value_basis, out_weight):
    gathered = lax.all_gather(latent, "seq", axis=1, tiled=True)
    attended_heads = attend(queries, gathered, key_basis, value_basis)
    partial_value = lax.dot_general(
        attended_heads,
        lax.all_gather(out_weight, "seq", axis=0, tiled=True),
        (((1,), (1,)), ((), ())),
        preferred_element_type=jnp.float32,
    )
    return lax.psum_scatter(partial_value, "head", scatter_dimension=1, tiled=True).astype(
        jnp.bfloat16
    )


def other_row(row, rows, j):
    reach = jnp.maximum(row, rows - 1 - row)
    below = row * 2 > rows - 1
    lone = jnp.abs(rows - 1 - 2 * row)
    k = j - lone
    distance = jnp.where(j < lone, reach - j, (reach - lone) - k // 2)
    towards_low = jnp.where(j < lone, below, (k % 2 == 0) == below)
    return jnp.where(towards_low, row - distance, row + distance)


def chunk_count(heads):
    return next(c for c in (4, 3, 2, 1) if heads % c == 0)


def kernel(
    n,
    q_hbm, lat_hbm, kb_hbm, vb_hbm, ow_hbm,
    out_ref,
    q_all, lat_all, kb, vb, ow, keys, values, early, part, swap, fin, landed,
    local_sem, send_sem, recv_sem, swap_sem, fin_send, fin_recv,
):
    chunks, _, tok, width = q_all.shape
    tokens = n * tok
    rows = n // 2
    heads = width // HEAD_DIM
    score_scale = 1.0 / math.sqrt(HEAD_DIM)
    me, core = lax.axis_index("seq"), lax.axis_index("head")
    row, side = me // 2, me % 2
    partner = row * 2 + (1 - side)

    def to(seq, head=core):
        return {"seq": seq, "head": head}

    half = lat_all.shape[3]
    mine = pl.ds(core * half, half)
    locals_ = [
        pltpu.make_async_copy(lat_hbm.at[:, mine], lat_all.at[core, me], local_sem.at[0]),
        pltpu.make_async_copy(kb_hbm, kb, local_sem.at[1]),
        pltpu.make_async_copy(vb_hbm, vb, local_sem.at[2]),
        pltpu.make_async_copy(ow_hbm, ow, local_sem.at[3]),
    ] + [
        pltpu.make_async_copy(
            q_hbm.at[:, pl.ds(c * width, width)], q_all.at[c, me], local_sem.at[4 + c]
        )
        for c in range(chunks)
    ]
    for copy in locals_:
        copy.start()

    barrier = pltpu.get_barrier_semaphore()
    others = [other_row(row, rows, j) for j in range(rows - 1)]
    greet = [to(r * 2 + x) for r in others for x in (side, 1 - side)]
    greet += [to(partner), to(me, 1 - core)]
    for peer in greet:
        pl.semaphore_signal(barrier, inc=1, device_id=peer, device_id_type=MESH)
    pl.semaphore_wait(barrier, len(greet))

    started = []

    def send(c, src, dst, seq, target, slot):
        copy = pltpu.make_async_remote_copy(
            src_ref=src,
            dst_ref=dst,
            send_sem=send_sem.at[c, slot],
            recv_sem=recv_sem.at[c, seq],
            device_id=to(target),
            device_id_type=MESH,
        )
        copy.start()
        started.append(copy)

    def arrived(c, seq):
        block = lat_all.at[core, seq] if c == chunks else q_all.at[c, seq]
        pltpu.make_async_remote_copy(
            src_ref=block,
            dst_ref=block,
            send_sem=send_sem.at[c, 0],
            recv_sem=recv_sem.at[c, seq],
            device_id=to(partner),
            device_id_type=MESH,
        ).wait_recv()

    peers = [r * 2 + x for r in others for x in (1 - side, side)] + [partner]
    for i, peer in enumerate(peers):
        send(chunks, lat_hbm.at[:, mine], lat_all.at[core, me], me, peer, i)
    for c in range(chunks):
        send(c, q_hbm.at[:, pl.ds(c * width, width)], q_all.at[c, me], me, partner, 0)
    relayed = max(chunks - DIRECT, 0)
    for c in range(chunks):
        src = q_hbm.at[:, pl.ds(c * width, width)]
        for j in range(rows - 1):
            if c >= relayed:
                send(c, src, q_all.at[c, me], me, others[j] * 2 + 1 - side, rows + j)
            send(c, src, q_all.at[c, me], me, others[j] * 2 + side, 1 + j)

    def relay(c):
        for j in range(rows - 1):
            seq = others[j] * 2 + side
            arrived(c, seq)
            if c < relayed:
                send(c, q_all.at[c, seq], q_all.at[c, seq], seq, partner, rows + j)

    for peer in peers:
        arrived(chunks, peer)
    locals_[0].wait()
    share = pltpu.make_async_remote_copy(
        src_ref=lat_all.at[core],
        dst_ref=lat_all.at[core],
        send_sem=swap_sem.at[2],
        recv_sem=swap_sem.at[3],
        device_id=to(me, 1 - core),
        device_id_type=MESH,
    )
    share.start()

    def decode(basis, which, c):
        return jnp.dot(
            lat_all[which].reshape(tokens, half),
            basis[pl.ds(which * half, half), pl.ds(c * width, width)],
            preferred_element_type=jnp.float32,
        )

    locals_[1].wait()
    locals_[2].wait()
    for c in range(chunks):
        early[0, c] = decode(kb, core, c)
        early[1, c] = decode(vb, core, c)
        if c < relayed - 1:
            relay(c)
    share.wait_recv()
    for c in range(chunks):
        keys[c] = (early[0, c] + decode(kb, 1 - core, c)).astype(jnp.bfloat16)
        values[c] = (early[1, c] + decode(vb, 1 - core, c)).astype(jnp.bfloat16)
    if relayed:
        relay(relayed - 1)

    locals_[3].wait()
    total = None
    for c in range(chunks):
        if c >= relayed:
            relay(c)
        for r in range(rows):
            arrived(c, r * 2 + 1 - side)
        locals_[4 + c].wait()
        mixed = []
        for h in range(heads):
            cols = pl.ds(h * HEAD_DIM, HEAD_DIM)
            query = q_all[c, :, :, cols].reshape(tokens, HEAD_DIM)
            scores = (
                lax.dot_general(
                    query,
                    keys[c, :, cols],
                    (((1,), (1,)), ((), ())),
                    preferred_element_type=jnp.float32,
                )
                * score_scale
            )
            weights = jnp.exp(scores - jnp.max(scores, axis=1, keepdims=True))
            totals = jnp.sum(weights, axis=1, keepdims=True)
            mixed.append(
                (
                    jnp.dot(
                        weights.astype(jnp.bfloat16),
                        values[c, :, cols],
                        preferred_element_type=jnp.float32,
                    )
                    / totals
                ).astype(jnp.bfloat16)
            )
        term = lax.dot_general(
            jnp.concatenate(mixed, axis=1) if heads > 1 else mixed[0],
            ow[:, pl.ds(c * width, width)],
            (((1,), (1,)), ((), ())),
            preferred_element_type=jnp.float32,
        )
        total = term if total is None else total + term

    part[...] = total.reshape(part.shape)
    exchange = pltpu.make_async_remote_copy(
        src_ref=part.at[1 - core],
        dst_ref=swap,
        send_sem=swap_sem.at[0],
        recv_sem=swap_sem.at[1],
        device_id=to(me, 1 - core),
        device_id_type=MESH,
    )
    exchange.start()
    exchange.wait_recv()
    fin[...] = (part[core] + swap[...]).astype(jnp.bfloat16).reshape(fin.shape)

    slot, keeper = me % rows, me // rows
    flip = me < core * rows + rows // 2
    for i in range(rows):
        j = jnp.where(flip, rows - 1 - i, i)
        owner = core * rows + j
        here = jnp.logical_and(owner == me, keeper == core)
        copy = pltpu.make_async_remote_copy(
            src_ref=fin.at[j],
            dst_ref=landed.at[slot],
            send_sem=fin_send.at[j],
            recv_sem=fin_recv.at[slot],
            device_id=to(owner, keeper),
            device_id_type=MESH,
        )

        @pl.when(jnp.logical_not(here))
        def _():
            copy.start()

        @pl.when(here)
        def _():
            landed[slot] = fin[j]

    own_here = me // rows == core
    feats = landed.shape[2]
    for i in range(rows):
        @pl.when(jnp.logical_not(jnp.logical_and(own_here, i == slot)))
        def _():
            pltpu.make_async_remote_copy(
                src_ref=landed.at[i],
                dst_ref=landed.at[i],
                send_sem=fin_send.at[0],
                recv_sem=fin_recv.at[i],
                device_id=to(partner),
                device_id_type=MESH,
            ).wait_recv()

        out_ref[:, i * feats : (i + 1) * feats] = landed[i]

    for copy in started:
        copy.wait_send()
    share.wait_send()
    exchange.wait_send()
    for j in range(rows):
        owner = core * rows + j

        @pl.when(jnp.logical_not(jnp.logical_and(owner == me, keeper == core)))
        def _():
            pltpu.make_async_remote_copy(
                src_ref=fin.at[j],
                dst_ref=landed.at[slot],
                send_sem=fin_send.at[j],
                recv_sem=fin_recv.at[slot],
                device_id=to(owner, keeper),
                device_id_type=MESH,
            ).wait_send()


def fused_shards(n, queries, latent, key_basis, value_basis, out_weight):
    tok, local = queries.shape
    rank = latent.shape[0]
    feats = out_weight.shape[0]
    chunks = chunk_count(local // HEAD_DIM)
    width = local // chunks
    rows = n // 2
    tokens = n * tok
    bf16, f32 = jnp.bfloat16, jnp.float32
    hbm = pl.BlockSpec(memory_space=pltpu.HBM)
    return pl.pallas_call(
        functools.partial(kernel, n),
        out_shape=jax.ShapeDtypeStruct((tok, rows * feats), bf16),
        in_specs=[hbm] * 5,
        out_specs=pl.BlockSpec(memory_space=pltpu.VMEM),
        scratch_shapes=[
            pltpu.VMEM((chunks, n, tok, width), bf16),
            pltpu.VMEM((2, n, tok, rank // 2), bf16),
            pltpu.VMEM((rank, local), bf16),
            pltpu.VMEM((rank, local), bf16),
            pltpu.VMEM((feats, local), bf16),
            pltpu.VMEM((chunks, tokens, width), bf16),
            pltpu.VMEM((chunks, tokens, width), bf16),
            pltpu.VMEM((2, chunks, tokens, width), f32),
            pltpu.VMEM((2, tokens // 2, feats), f32),
            pltpu.VMEM((tokens // 2, feats), f32),
            pltpu.VMEM((rows, tok, feats), bf16),
            pltpu.VMEM((rows, tok, feats), bf16),
            pltpu.SemaphoreType.DMA((4 + chunks,)),
            pltpu.SemaphoreType.DMA((chunks + 1, n)),
            pltpu.SemaphoreType.DMA((chunks + 1, n)),
            pltpu.SemaphoreType.DMA((4,)),
            pltpu.SemaphoreType.DMA((rows,)),
            pltpu.SemaphoreType.DMA((rows,)),
        ],
        compiler_params=pltpu.CompilerParams(
            collective_id=0, has_side_effects=True, vmem_limit_bytes=VMEM_BUDGET
        ),
        name="fused_attention",
    )(*(
        pltpu.with_memory_space_constraint(x, pltpu.HBM)
        for x in (queries, latent.T, key_basis, value_basis, out_weight)
    ))


def shards(n, cores, queries, latent, key_basis, value_basis, out_weight):
    tok, local = queries.shape
    rank = latent.shape[0]
    feats = out_weight.shape[0]
    tokens = n * tok
    held = 2 * (3 * tokens * local + tokens * rank + 2 * rank * local + feats * local)
    held += 4 * (2 * tokens * local + 3 * tokens * feats + 3 * tokens * tokens)
    if (
        cores == 2
        and n % 2 == 0
        and tok % 16 == 0
        and feats % 128 == 0
        and rank % 256 == 0
        and held <= VMEM_BUDGET
    ):
        return fused_shards(n, queries, latent, key_basis, value_basis, out_weight)
    return collective_shards(queries, latent, key_basis, value_basis, out_weight)


def solution(mesh):
    placed = (
        P(("groups", "seq"), "head"),
        P(None, ("groups", "seq")),
        P(None, "head"),
        P(None, "head"),
        P("seq", "head"),
    )
    return jax.shard_map(
        functools.partial(shards, mesh.shape["seq"], mesh.shape["head"]),
        mesh=mesh,
        in_specs=placed,
        out_specs=P(("groups", "seq"), "head"),
        check_vma=False,
    )
```

```python
import functools
import math

import jax
import jax.numpy as jnp
from jax import lax
from jax.experimental import pallas as pl
from jax.experimental.pallas import tpu as pltpu
from jax.sharding import PartitionSpec as P

HEAD_DIM = 128
MESH = pl.DeviceIdType.MESH
VMEM_BUDGET = 40 * 2**20
DIRECT = 0


def attend(queries, latent, key_basis, value_basis):
    tok_rows = queries.shape[0]
    head_count = key_basis.shape[1] // HEAD_DIM
    rank_count = key_basis.shape[0]
    score_scale = 1.0 / math.sqrt(HEAD_DIM)
    query_heads = queries.reshape(tok_rows, head_count, HEAD_DIM).transpose(1, 0, 2)
    key_maps = key_basis.reshape(rank_count, head_count, HEAD_DIM).transpose(1, 0, 2)
    value_maps = value_basis.reshape(rank_count, head_count, HEAD_DIM).transpose(1, 0, 2)

    def one_head(operands):
        query_one, key_map, value_map = operands
        key_rows = lax.dot_general(
            latent, key_map, (((0,), (0,)), ((), ())), preferred_element_type=jnp.float32
        ).astype(jnp.bfloat16)
        value_rows = lax.dot_general(
            latent, value_map, (((0,), (0,)), ((), ())), preferred_element_type=jnp.float32
        ).astype(jnp.bfloat16)
        scores = (
            lax.dot_general(
                query_one, key_rows, (((1,), (1,)), ((), ())), preferred_element_type=jnp.float32
            )
            * score_scale
        )
        row_max = jnp.max(scores, axis=1, keepdims=True)
        weights = jnp.exp(scores - row_max)
        row_total = jnp.sum(weights, axis=1, keepdims=True)
        head_mixed = (
            jnp.dot(weights.astype(jnp.bfloat16), value_rows, preferred_element_type=jnp.float32)
            / row_total
        )
        return head_mixed.astype(jnp.bfloat16)

    mixed = lax.map(one_head, (query_heads, key_maps, value_maps))
    return mixed.transpose(1, 0, 2).reshape(tok_rows, head_count * HEAD_DIM)


def collective_shards(queries, latent, key_basis, value_basis, out_weight):
    gathered = lax.all_gather(latent, "seq", axis=1, tiled=True)
    attended_heads = attend(queries, gathered, key_basis, value_basis)
    partial_value = lax.dot_general(
        attended_heads,
        lax.all_gather(out_weight, "seq", axis=0, tiled=True),
        (((1,), (1,)), ((), ())),
        preferred_element_type=jnp.float32,
    )
    return lax.psum_scatter(partial_value, "head", scatter_dimension=1, tiled=True).astype(
        jnp.bfloat16
    )


def other_row(row, rows, j):
    reach = jnp.maximum(row, rows - 1 - row)
    below = row * 2 > rows - 1
    lone = jnp.abs(rows - 1 - 2 * row)
    k = j - lone
    distance = jnp.where(j < lone, reach - j, (reach - lone) - k // 2)
    towards_low = jnp.where(j < lone, below, (k % 2 == 0) == below)
    return jnp.where(towards_low, row - distance, row + distance)


def chunk_count(heads):
    return next(c for c in (4, 3, 2, 1) if heads % c == 0)


def kernel(
    n,
    q_hbm, lat_hbm, kb_hbm, vb_hbm, ow_hbm,
    out_ref,
    q_all, lat_all, kb, vb, ow, keys, values, early, part, swap, fin, landed,
    local_sem, send_sem, recv_sem, swap_sem, fin_send, fin_recv,
):
    chunks, _, tok, width = q_all.shape
    tokens = n * tok
    rows = n // 2
    heads = width // HEAD_DIM
    score_scale = 1.0 / math.sqrt(HEAD_DIM)
    me, core = lax.axis_index("seq"), lax.axis_index("head")
    row, side = me // 2, me % 2
    partner = row * 2 + (1 - side)

    def to(seq, head=core):
        return {"seq": seq, "head": head}

    half = lat_all.shape[3]
    mine = pl.ds(core * half, half)
    locals_ = [
        pltpu.make_async_copy(lat_hbm.at[:, mine], lat_all.at[core, me], local_sem.at[0]),
        pltpu.make_async_copy(kb_hbm, kb, local_sem.at[1]),
        pltpu.make_async_copy(vb_hbm, vb, local_sem.at[2]),
        pltpu.make_async_copy(ow_hbm, ow, local_sem.at[3]),
    ] + [
        pltpu.make_async_copy(
            q_hbm.at[:, pl.ds(c * width, width)], q_all.at[c, me], local_sem.at[4 + c]
        )
        for c in range(chunks)
    ]
    barrier = pltpu.get_barrier_semaphore()
    others = [other_row(row, rows, j) for j in range(rows - 1)]
    greet = [to(r * 2 + x) for r in others for x in (side, 1 - side)]
    greet += [to(partner), to(me, 1 - core)]
    for peer in greet:
        pl.semaphore_signal(barrier, inc=1, device_id=peer, device_id_type=MESH)
    for copy in locals_:
        copy.start()
    pl.semaphore_wait(barrier, len(greet))

    started = []

    def send(c, src, dst, seq, target, slot):
        copy = pltpu.make_async_remote_copy(
            src_ref=src,
            dst_ref=dst,
            send_sem=send_sem.at[c, slot],
            recv_sem=recv_sem.at[c, seq],
            device_id=to(target),
            device_id_type=MESH,
        )
        copy.start()
        started.append(copy)

    def arrived(c, seq):
        block = lat_all.at[core, seq] if c == chunks else q_all.at[c, seq]
        pltpu.make_async_remote_copy(
            src_ref=block,
            dst_ref=block,
            send_sem=send_sem.at[c, 0],
            recv_sem=recv_sem.at[c, seq],
            device_id=to(partner),
            device_id_type=MESH,
        ).wait_recv()

    peers = [r * 2 + x for r in others for x in (1 - side, side)] + [partner]
    for i, peer in enumerate(peers):
        send(chunks, lat_hbm.at[:, mine], lat_all.at[core, me], me, peer, i)
    for c in range(chunks):
        send(c, q_hbm.at[:, pl.ds(c * width, width)], q_all.at[c, me], me, partner, 0)
    relayed = max(chunks - DIRECT, 0)
    for c in range(chunks):
        src = q_hbm.at[:, pl.ds(c * width, width)]
        for j in range(rows - 1):
            if c >= relayed:
                send(c, src, q_all.at[c, me], me, others[j] * 2 + 1 - side, rows + j)
            send(c, src, q_all.at[c, me], me, others[j] * 2 + side, 1 + j)

    def relay(c):
        for j in reversed(range(rows - 1)):
            seq = others[j] * 2 + side
            arrived(c, seq)
            if c < relayed:
                send(c, q_all.at[c, seq], q_all.at[c, seq], seq, partner, rows + j)

    for peer in peers:
        arrived(chunks, peer)
    locals_[0].wait()
    share = pltpu.make_async_remote_copy(
        src_ref=lat_all.at[core],
        dst_ref=lat_all.at[core],
        send_sem=swap_sem.at[2],
        recv_sem=swap_sem.at[3],
        device_id=to(me, 1 - core),
        device_id_type=MESH,
    )
    share.start()

    def decode(basis, which, c):
        return jnp.dot(
            lat_all[which].reshape(tokens, half),
            basis[pl.ds(which * half, half), pl.ds(c * width, width)],
            preferred_element_type=jnp.float32,
        )

    locals_[1].wait()
    locals_[2].wait()
    for c in range(chunks):
        early[0, c] = decode(kb, core, c)
        early[1, c] = decode(vb, core, c)
        if c < relayed - 1:
            relay(c)
    share.wait_recv()
    for c in range(chunks):
        keys[c] = (early[0, c] + decode(kb, 1 - core, c)).astype(jnp.bfloat16)
        values[c] = (early[1, c] + decode(vb, 1 - core, c)).astype(jnp.bfloat16)
    if relayed:
        relay(relayed - 1)

    locals_[3].wait()
    total = None
    for c in range(chunks):
        if c >= relayed:
            relay(c)
        for r in range(rows):
            arrived(c, r * 2 + 1 - side)
        locals_[4 + c].wait()
        mixed = []
        for h in range(heads):
            cols = pl.ds(h * HEAD_DIM, HEAD_DIM)
            query = q_all[c, :, :, cols].reshape(tokens, HEAD_DIM)
            scores = (
                lax.dot_general(
                    query,
                    keys[c, :, cols],
                    (((1,), (1,)), ((), ())),
                    preferred_element_type=jnp.float32,
                )
                * score_scale
            )
            weights = jnp.exp(scores - jnp.max(scores, axis=1, keepdims=True))
            totals = jnp.sum(weights, axis=1, keepdims=True)
            mixed.append(
                (
                    jnp.dot(
                        weights.astype(jnp.bfloat16),
                        values[c, :, cols],
                        preferred_element_type=jnp.float32,
                    )
                    / totals
                ).astype(jnp.bfloat16)
            )
        term = lax.dot_general(
            jnp.concatenate(mixed, axis=1) if heads > 1 else mixed[0],
            ow[:, pl.ds(c * width, width)],
            (((1,), (1,)), ((), ())),
            preferred_element_type=jnp.float32,
        )
        total = term if total is None else total + term

    part[...] = total.reshape(part.shape)
    exchange = pltpu.make_async_remote_copy(
        src_ref=part.at[1 - core],
        dst_ref=swap,
        send_sem=swap_sem.at[0],
        recv_sem=swap_sem.at[1],
        device_id=to(me, 1 - core),
        device_id_type=MESH,
    )
    exchange.start()
    exchange.wait_recv()
    fin[...] = (part[core] + swap[...]).astype(jnp.bfloat16).reshape(fin.shape)

    slot, keeper = me % rows, me // rows
    flip = me < core * rows + rows // 2
    for i in range(rows):
        j = jnp.where(flip, rows - 1 - i, i)
        owner = core * rows + j
        here = jnp.logical_and(owner == me, keeper == core)
        copy = pltpu.make_async_remote_copy(
            src_ref=fin.at[j],
            dst_ref=landed.at[slot],
            send_sem=fin_send.at[j],
            recv_sem=fin_recv.at[slot],
            device_id=to(owner, keeper),
            device_id_type=MESH,
        )

        @pl.when(jnp.logical_not(here))
        def _():
            copy.start()

        @pl.when(here)
        def _():
            landed[slot] = fin[j]

    own_here = me // rows == core
    feats = landed.shape[2]
    for i in range(rows):
        @pl.when(jnp.logical_not(jnp.logical_and(own_here, i == slot)))
        def _():
            pltpu.make_async_remote_copy(
                src_ref=landed.at[i],
                dst_ref=landed.at[i],
                send_sem=fin_send.at[0],
                recv_sem=fin_recv.at[i],
                device_id=to(partner),
                device_id_type=MESH,
            ).wait_recv()

        out_ref[:, i * feats : (i + 1) * feats] = landed[i]

    for copy in started:
        copy.wait_send()
    share.wait_send()
    exchange.wait_send()
    for j in range(rows):
        owner = core * rows + j

        @pl.when(jnp.logical_not(jnp.logical_and(owner == me, keeper == core)))
        def _():
            pltpu.make_async_remote_copy(
                src_ref=fin.at[j],
                dst_ref=landed.at[slot],
                send_sem=fin_send.at[j],
                recv_sem=fin_recv.at[slot],
                device_id=to(owner, keeper),
                device_id_type=MESH,
            ).wait_send()


def fused_shards(n, queries, latent, key_basis, value_basis, out_weight):
    tok, local = queries.shape
    rank = latent.shape[0]
    feats = out_weight.shape[0]
    chunks = chunk_count(local // HEAD_DIM)
    width = local // chunks
    rows = n // 2
    tokens = n * tok
    bf16, f32 = jnp.bfloat16, jnp.float32
    hbm = pl.BlockSpec(memory_space=pltpu.HBM)
    return pl.pallas_call(
        functools.partial(kernel, n),
        out_shape=jax.ShapeDtypeStruct((tok, rows * feats), bf16),
        in_specs=[hbm] * 5,
        out_specs=pl.BlockSpec(memory_space=pltpu.VMEM),
        scratch_shapes=[
            pltpu.VMEM((chunks, n, tok, width), bf16),
            pltpu.VMEM((2, n, tok, rank // 2), bf16),
            pltpu.VMEM((rank, local), bf16),
            pltpu.VMEM((rank, local), bf16),
            pltpu.VMEM((feats, local), bf16),
            pltpu.VMEM((chunks, tokens, width), bf16),
            pltpu.VMEM((chunks, tokens, width), bf16),
            pltpu.VMEM((2, chunks, tokens, width), f32),
            pltpu.VMEM((2, tokens // 2, feats), f32),
            pltpu.VMEM((tokens // 2, feats), f32),
            pltpu.VMEM((rows, tok, feats), bf16),
            pltpu.VMEM((rows, tok, feats), bf16),
            pltpu.SemaphoreType.DMA((4 + chunks,)),
            pltpu.SemaphoreType.DMA((chunks + 1, n)),
            pltpu.SemaphoreType.DMA((chunks + 1, n)),
            pltpu.SemaphoreType.DMA((4,)),
            pltpu.SemaphoreType.DMA((rows,)),
            pltpu.SemaphoreType.DMA((rows,)),
        ],
        compiler_params=pltpu.CompilerParams(
            collective_id=0, has_side_effects=True, vmem_limit_bytes=VMEM_BUDGET
        ),
        name="fused_attention",
    )(*(
        pltpu.with_memory_space_constraint(x, pltpu.HBM)
        for x in (queries, latent.T, key_basis, value_basis, out_weight)
    ))


def shards(n, cores, queries, latent, key_basis, value_basis, out_weight):
    tok, local = queries.shape
    rank = latent.shape[0]
    feats = out_weight.shape[0]
    tokens = n * tok
    held = 2 * (3 * tokens * local + tokens * rank + 2 * rank * local + feats * local)
    held += 4 * (2 * tokens * local + 3 * tokens * feats + 3 * tokens * tokens)
    if (
        cores == 2
        and n % 2 == 0
        and tok % 16 == 0
        and feats % 128 == 0
        and rank % 256 == 0
        and held <= VMEM_BUDGET
    ):
        return fused_shards(n, queries, latent, key_basis, value_basis, out_weight)
    return collective_shards(queries, latent, key_basis, value_basis, out_weight)


def solution(mesh):
    placed = (
        P(("groups", "seq"), "head"),
        P(None, ("groups", "seq")),
        P(None, "head"),
        P(None, "head"),
        P("seq", "head"),
    )
    return jax.shard_map(
        functools.partial(shards, mesh.shape["seq"], mesh.shape["head"]),
        mesh=mesh,
        in_specs=placed,
        out_specs=P(("groups", "seq"), "head"),
        check_vma=False,
    )
```
